128 devices in a mesh: expert: 8 (over z_lo, x), shard: 16 (over z_hi, y, core).
Axes of the slice: x: 4, y: 4, z: 4 (z_hi: 2, z_lo: 2; z = z_hi * 2 + z_lo), core: 2. Of those that a mesh axis runs over, the one named last changes fastest.
Arguments:
- tokens: bfloat16 [1024, 4096], P('expert', 'shard'), may hold values from -6 to 6
- routes: int32 [1024, 2], P('expert'), may hold values from 0 to 7, all different within a row; in each aligned block of 128 rows (0 to 127, 128 to 255, ...) at most 96 rows name the same one
- mix_weights: float32 [1024, 2], P('expert'), may hold values from 0.1 to 1
- cotangent: bfloat16 [1024, 4096], P('expert', 'shard'), may hold values from -6 to 6
- w_gate: bfloat16 [8, 4096, 6144], P('expert', 'shard'), may hold values from -0.09375 to 0.09375
- w_up: bfloat16 [8, 4096, 6144], P('expert', 'shard'), may hold values from -0.09375 to 0.09375
- w_down: bfloat16 [8, 4096, 6144], P('expert', 'shard'), may hold values from -0.078125 to 0.078125
Outputs:
- layer_out: bfloat16 [1024, 4096], P('expert', 'shard')
- grad_tokens: bfloat16 [1024, 4096], P('expert', 'shard')
- grad_gate: bfloat16 [8, 4096, 6144], P('expert', None, 'shard')
- grad_up: bfloat16 [8, 4096, 6144], P('expert', None, 'shard')
- grad_down: bfloat16 [8, 4096, 6144], P('expert', None, 'shard')
The draws below stay inside these ranges and needn't reach their ends.
Inputs may be any that keep to these rules, and one draw needn't show every extreme that they name: `routes`: each token names two different experts. Among the 128 tokens of one block, no expert is named by more than 96 tokens, and in every draw some expert is named by exactly 96 tokens of some block. Every expert is named by some token.
All inputs are finite; a program needn't handle non-finite values.
Results may differ from the reference program's by a relative error of at most 0.015.
Values may be sent and summed in bfloat16 or wider, within the bound.
No kernel may reach another device: no remote copies, remote signals or barrier semaphores. Data moves between devices by JAX's collectives and lax.ppermute only.
A program may use at most 128 MiB of HBM per device.

```python
import math
import jax
import jax.numpy as jnp
import numpy as np
from jax import lax

D = 4096
FFW = 6144
TOK_DEV = 128
EXPERTS = 8
CAP = 96
TOKENS = 1024
N_EXPERT = 8
N_SHARD = 16


def block_scale(key, extent, pieces, smallest, largest):
    loudness, own = 1.0, jax.random.fold_in(key, 6)
    for dim, parts in pieces:
        draws = jnp.exp(jax.random.uniform(jax.random.fold_in(own, dim), (parts,), jnp.float32, smallest / len(pieces), largest / len(pieces)))
        loudness = loudness * jnp.repeat(draws, extent[dim] // parts).reshape([-1 if axis == dim else 1 for axis in range(len(extent))])
    return loudness


def deal_out(stream_key, own, number, rows, number_of, top, reach, slope):
    sequence = jax.random.permutation(stream_key, number_of)
    heavy_load, usual = shares(number_of, rows * top, reach, slope, True), shares(number_of, rows * top, reach, slope, False)
    places = jnp.arange(number_of)

    def named(lengths, rotation):
        used = int((lengths > 0).sum())
        fixed = max(1, used // 4)
        shifted = fixed + (places - fixed + rotation * (used - fixed)) % max(1, number_of - fixed)
        return jnp.zeros((number_of,), jnp.int32).at[sequence[jnp.where(places < fixed, places, shifted)]].set(jnp.asarray(lengths, jnp.int32))

    lengths = jnp.where(number % 4 == 0, named(heavy_load, number // 4), named(usual, number - number // 4 - 1))
    mixed = jax.random.permutation(jax.random.fold_in(own, 3), number_of)
    source_of, taker = mixed[0:number_of // 2 * 2:2], mixed[1:number_of // 2 * 2:2]
    room = jnp.minimum(lengths[source_of] - 1, reach - lengths[taker]) // 2
    room = jnp.where((source_of == sequence[0]) | (taker == sequence[0]) | (lengths[taker] == 0), 0, jnp.maximum(room, 0))
    shifted = jax.random.randint(jax.random.fold_in(own, 4), (number_of // 2,), 0, 1 << 20) % (room + 1)
    lengths = lengths.at[source_of].add(-shifted).at[taker].add(shifted)
    labels = jnp.searchsorted(jnp.cumsum(lengths), jnp.arange(rows * top), side="right").astype(jnp.int32)
    table = labels.reshape(top, rows).T
    table = table[jax.random.permutation(jax.random.fold_in(own, 1), rows)]
    rotation = jax.random.randint(jax.random.fold_in(own, 2), (rows, 1), 0, top)
    return jnp.take_along_axis(table, (jnp.arange(top)[None, :] + rotation) % top, axis=1)


def shares(amount, total, most, slope, full):
    weights = [(1 << 20) // math.isqrt(rank ** slope) + 1 for rank in range(1, amount + 1)]
    largest = most if full else min(most, max(-(-total // amount), total * weights[0] // sum(weights)))
    least = 1 if total - largest >= amount - 1 else 0
    counts, spare = [largest] + [least] * (amount - 1), total - largest - least * (amount - 1)
    while spare > 0:
        movable = [i for i in range(1, amount) if counts[i] < largest] or [i for i in range(1, amount) if counts[i] < most]
        mass, left = sum([weights[i] for i in movable]), spare
        for i in movable:
            addition = min(most - counts[i], max(1, left * weights[i] // mass), spare)
            counts[i] = counts[i] + addition
            spare = spare - addition
    return np.array(counts)


def scatter_about(stream_key, shape, deviation, reach, pieces=(), kind=jnp.bfloat16):
    drawn = jax.random.normal(stream_key, shape, jnp.float32) * deviation
    if len(pieces) > 0:
        drawn = block_scale(stream_key, shape, pieces, -0.22, 0.18) * drawn
    return jnp.clip(drawn, min=-reach, max=reach).astype(kind)


def setup_inputs(seed: int = 0) -> dict:
    splits = jax.random.split(jax.random.key(seed), 8)
    tokens = scatter_about(splits[0], (TOKENS, D), 1.0, 6.0, ((0, 8), (1, 16)))
    routes_keys = jax.random.split(jax.random.fold_in(splits[1], 1), TOKENS // TOK_DEV)
    routes_turns = jax.random.permutation(jax.random.fold_in(splits[1], 3), TOKENS // TOK_DEV)
    routes = jax.vmap(lambda own, number: deal_out(jax.random.fold_in(splits[1], 2), own, number, TOK_DEV, EXPERTS, 2, CAP, 2))(routes_keys, routes_turns).reshape((TOKENS, 2))
    mix_weights = jnp.clip(0.1 + 0.9 * jax.random.uniform(splits[2], (TOKENS, 2), jnp.float32) ** block_scale(splits[2], (TOKENS, 2), ((0, 8),), -0.2, 0.2), 0.1, 1.0)
    cotangent = scatter_about(splits[3], (TOKENS, D), 1.0, 6.0, ((0, 8), (1, 16)))
    w_gate = scatter_about(splits[4], (EXPERTS, D, FFW), D ** -0.5, 0.09375, ((0, 8), (1, 16)))
    w_up = scatter_about(splits[5], (EXPERTS, D, FFW), D ** -0.5, 0.09375, ((0, 8), (1, 16)))
    w_down = scatter_about(splits[6], (EXPERTS, D, FFW), FFW ** -0.5, 0.078125, ((0, 8), (1, 16)))
    return dict(tokens=tokens, routes=routes, mix_weights=mix_weights, cotangent=cotangent, w_gate=w_gate, w_up=w_up, w_down=w_down)


def target_rows(routes):
    grouped = routes.reshape(N_EXPERT, TOK_DEV * 2)
    expert_iota = jnp.arange(EXPERTS, dtype=jnp.int32)
    one_hot = (grouped[:, :, None] == expert_iota[None, None, :]).astype(jnp.int32)
    earlier = jnp.cumsum(one_hot, axis=1) - one_hot
    slot_number = jnp.sum(earlier * one_hot, axis=2)
    source = jnp.arange(N_EXPERT, dtype=jnp.int32)[:, None]
    target = grouped * (N_EXPERT * CAP) + source * CAP + slot_number
    return target.reshape(TOKENS, 2).astype(jnp.int32)


def expert_pass(inputs):
    rows_in, grads_in, gate_w, up_w, down_w = inputs
    gate_pre = jnp.dot(rows_in, gate_w, preferred_element_type=jnp.float32)
    up_pre = jnp.dot(rows_in, up_w, preferred_element_type=jnp.float32)
    sigmoid_gate = jax.nn.sigmoid(gate_pre)
    active = gate_pre * sigmoid_gate
    hidden = (active * up_pre).astype(jnp.bfloat16)
    d_hidden = jnp.dot(grads_in, down_w, preferred_element_type=jnp.float32)
    d_gate = (d_hidden * up_pre * sigmoid_gate * (1.0 + gate_pre * (1.0 - sigmoid_gate))).astype(jnp.bfloat16)
    d_up = (d_hidden * active).astype(jnp.bfloat16)
    piece_width = FFW // N_SHARD
    row_count = rows_in.shape[0]

    def one_shard(totals, piece_index):
        carry_out, carry_dx = totals
        first_col = (piece_index * piece_width).astype(jnp.int32)
        hid_piece = lax.dynamic_slice_in_dim(hidden, first_col, piece_width, 1)
        down_piece = lax.dynamic_slice_in_dim(down_w, first_col, piece_width, 1)
        gate_piece = lax.dynamic_slice_in_dim(gate_w, first_col, piece_width, 1)
        up_piece = lax.dynamic_slice_in_dim(up_w, first_col, piece_width, 1)
        dg_piece = lax.dynamic_slice_in_dim(d_gate, first_col, piece_width, 1)
        du_piece = lax.dynamic_slice_in_dim(d_up, first_col, piece_width, 1)
        out_part = jnp.dot(hid_piece, down_piece.T, preferred_element_type=jnp.float32)
        dx_part = jnp.dot(dg_piece, gate_piece.T, preferred_element_type=jnp.float32)
        dx_part = dx_part + jnp.dot(du_piece, up_piece.T, preferred_element_type=jnp.float32)
        out_round = lax.optimization_barrier(out_part.astype(jnp.bfloat16)).astype(jnp.float32)
        dx_round = lax.optimization_barrier(dx_part.astype(jnp.bfloat16)).astype(jnp.float32)
        return (carry_out + out_round, carry_dx + dx_round), None

    zeros_rows = jnp.zeros((row_count, D), jnp.float32)
    totals, unused = lax.scan(one_shard, (zeros_rows, zeros_rows), jnp.arange(N_SHARD, dtype=jnp.int32))
    out_rows = totals[0].astype(jnp.bfloat16)
    dx_rows = totals[1].astype(jnp.bfloat16)
    grad_gate = jnp.dot(rows_in.T, d_gate, preferred_element_type=jnp.float32).astype(jnp.bfloat16)
    grad_up = jnp.dot(rows_in.T, d_up, preferred_element_type=jnp.float32).astype(jnp.bfloat16)
    grad_down = jnp.dot(grads_in.T, hidden, preferred_element_type=jnp.float32).astype(jnp.bfloat16)
    return out_rows, dx_rows, grad_gate, grad_up, grad_down


def reference(tokens, routes, mix_weights, cotangent, w_gate, w_up, w_down):
    target = target_rows(routes)
    flat_target = target.reshape(-1)
    token_index = jnp.repeat(jnp.arange(TOKENS, dtype=jnp.int32), 2)
    total_rows = EXPERTS * N_EXPERT * CAP
    sent_rows = jnp.zeros((total_rows, D), jnp.bfloat16).at[flat_target].set(tokens[token_index])
    scaled = (mix_weights[:, :, None] * cotangent[:, None, :].astype(jnp.float32)).astype(jnp.bfloat16)
    sent_grads = jnp.zeros((total_rows, D), jnp.bfloat16).at[flat_target].set(scaled.reshape(TOKENS * 2, D))
    results = lax.map(expert_pass, (sent_rows.reshape(EXPERTS, N_EXPERT * CAP, D), sent_grads.reshape(EXPERTS, N_EXPERT * CAP, D), w_gate, w_up, w_down))
    out_rows, dx_rows, grad_gate, grad_up, grad_down = results
    picked = out_rows.reshape(total_rows, D)[target]
    layer_out = jnp.sum(mix_weights[:, :, None] * picked.astype(jnp.float32), axis=1).astype(jnp.bfloat16)
    picked_dx = dx_rows.reshape(total_rows, D)[target]
    grad_tokens = jnp.sum(picked_dx.astype(jnp.float32), axis=1).astype(jnp.bfloat16)
    return layer_out, grad_tokens, grad_gate, grad_up, grad_down
```

```python
import jax
import jax.numpy as jnp
from jax import lax
from jax.experimental import pallas as pl
from jax.experimental.pallas import tpu as pltpu
from jax.sharding import Mesh, PartitionSpec as P


EXPERT = ("z_lo", "x")
SHARD = ("z_hi", "y", "core")
N_X, N_CHIP = 4, 8


def swap(value, axes, size, offset):
    return lax.ppermute(value, axes, [(i, i ^ offset) for i in range(size)])


def chip_swap(value, k):
    return swap(value, ("z_hi", "y"), N_CHIP, k)


def core_swap(value):
    return swap(value, "core", 2, 1)


def dot(a, b, contract):
    return lax.dot_general(a, b, ((contract[0], contract[1]), ((), ())), preferred_element_type=jnp.float32)


def pack(weights, shard):
    rows, hidden = weights[0].shape
    parts = 2 * N_CHIP
    piece = hidden // parts
    step = rows // 2

    def kernel(shard_ref, *refs):
        ins, out = refs[:-1], refs[-1]
        for d in range(parts):
            rel = jnp.bitwise_xor(shard_ref[0], d)
            for n, ref in enumerate(ins):
                out[rel % 2, rel // 2, :, n * piece : (n + 1) * piece] = ref[:, d * piece : (d + 1) * piece]

    width = piece * len(weights)
    return pl.pallas_call(
        kernel,
        grid_spec=pltpu.PrefetchScalarGridSpec(
            num_scalar_prefetch=1,
            grid=(rows // step,),
            in_specs=[pl.BlockSpec((step, hidden), lambda i, s: (i, 0)) for _ in weights],
            out_specs=pl.BlockSpec((2, N_CHIP, step, width), lambda i, s: (0, 0, i, 0)),
        ),
        out_shape=jax.ShapeDtypeStruct((2, N_CHIP, rows, width), weights[0].dtype),
        name="pack",
    )(shard, *weights)


def exchange(packed):
    other = core_swap(packed[1])
    pieces = [jnp.stack([packed[0, k], other[k]]) for k in range(N_CHIP)]
    moved = [pieces[0]] + [chip_swap(pieces[k], k) for k in range(1, N_CHIP)]
    rows, width = packed.shape[2:]
    return [jnp.concatenate([m[b] for m in moved], axis=0) for b in range(2)]


def weight_grad(own, other, right, shard, n_out):
    rows, half = own.shape
    piece = half // N_CHIP
    width = right.shape[1] // n_out

    def kernel(shard_ref, own_ref, other_ref, right_ref, *outs):
        core = shard_ref[0] % 2
        for ref, place in ((own_ref, core), (other_ref, 1 - core)):
            total = dot(ref[...], right_ref[...], ((0,), (0,))).astype(outs[0].dtype)
            at = pl.ds(pl.multiple_of(place * piece, piece), piece)
            for n, out in enumerate(outs):
                out[0, at, :] = total[:, n * width : (n + 1) * width]

    in_block = pl.BlockSpec((rows, piece), lambda k, s: (0, k))
    out_block = pl.BlockSpec((1, 2 * piece, width), lambda k, s: (0, jnp.bitwise_xor(s[0] // 2, k), 0))
    return pl.pallas_call(
        kernel,
        grid_spec=pltpu.PrefetchScalarGridSpec(
            num_scalar_prefetch=1,
            grid=(N_CHIP,),
            in_specs=[in_block, in_block, pl.BlockSpec(right.shape, lambda k, s: (0, 0))],
            out_specs=[out_block] * n_out,
        ),
        out_shape=[jax.ShapeDtypeStruct((1, 2 * half, width), jnp.bfloat16)] * n_out,
        cost_estimate=pl.CostEstimate(
            flops=4 * rows * half * right.shape[1],
            bytes_accessed=4 * rows * half + 2 * right.size + 4 * half * right.shape[1],
            transcendentals=0,
        ),
        name="weight_grad",
    )(shard, own, other, right)


def slots_of(routes):
    flat = routes.reshape(-1)
    one_hot = (flat[:, None] == jnp.arange(2 * N_X, dtype=jnp.int32)[None, :]).astype(jnp.int32)
    earlier = jnp.cumsum(one_hot, axis=0) - one_hot
    return jnp.sum(earlier * one_hot, axis=1).reshape(routes.shape)


def hits(routes, slots, experts, capacity):
    row_slot = jnp.tile(jnp.arange(capacity, dtype=jnp.int32), len(experts))
    row_expert = jnp.repeat(jnp.stack(experts), capacity)
    return (row_expert[:, None, None] == routes[None]) & (row_slot[:, None, None] == slots[None])


def feature_sum(own, other, groups):
    mine = own + core_swap(other.astype(jnp.bfloat16)).astype(jnp.float32)
    piece = own.shape[1] // N_CHIP
    parts = [mine[:, k * piece : (k + 1) * piece] for k in range(N_CHIP)]
    moved = [chip_swap(parts[k].astype(jnp.bfloat16), k) for k in range(1, N_CHIP)]
    total = parts[0]
    for m in moved:
        total = total + m.astype(jnp.float32)
    return send_home(total.astype(jnp.bfloat16), groups)


def send_home(rows, capacity):
    width = rows.shape[1]
    shaped = rows.reshape(N_X, 2, capacity, width)
    back = [shaped[0]] + [swap(shaped[d], "x", N_X, d) for d in range(1, N_X)]
    back = jnp.stack(back, axis=1)
    crossed = swap(back[1], "z_lo", 2, 1)
    return jnp.concatenate([back[0].reshape(-1, width), crossed.reshape(-1, width)], axis=0)


def local(tokens, routes, mix_weights, cotangent, w_gate, w_up, w_down):
    tok_dev, piece_width = tokens.shape
    capacity = min(tok_dev, 6 * tok_dev // (2 * N_X))
    z_lo, x = lax.axis_index("z_lo"), lax.axis_index("x")
    shard = lax.axis_index(SHARD).astype(jnp.int32)[None]

    packed_gu = pack([w_gate[0], w_up[0]], shard)
    packed_down = pack([w_down[0]], shard)

    info = jnp.concatenate([routes.astype(jnp.float32), mix_weights], axis=1)
    info_other = swap(info, "z_lo", 2, 1)
    pair = jnp.stack([tokens, cotangent])
    both = jnp.stack([pair, swap(pair, "z_lo", 2, 1)])
    gathered = [both] + [chip_swap(both, k) for k in range(1, N_CHIP)]

    gu_own, gu_other = exchange(packed_gu)
    down_own, down_other = exchange(packed_down)

    experts = [z_lo * N_X + jnp.bitwise_xor(x, d) for d in range(N_X)]
    row_sets, grad_sets = [], []
    for block, block_info in enumerate((info, info_other)):
        block_routes = block_info[:, :2].astype(jnp.int32)
        found = hits(block_routes, slots_of(block_routes), experts, capacity)
        picker = jnp.any(found, axis=2).astype(jnp.bfloat16)
        weight = jnp.sum(jnp.where(found, block_info[None, :, 2:], 0.0), axis=(1, 2))
        features = [jnp.concatenate([g[block, n] for g in gathered], axis=1) for n in range(2)]
        row_sets.append(dot(picker, features[0], ((1,), (0,))).astype(jnp.bfloat16))
        grad_sets.append((dot(picker, features[1], ((1,), (0,))) * weight[:, None]).astype(jnp.bfloat16))

    def to_owner(sets):
        own = []
        for d in range(N_X):
            part = jnp.concatenate([s[d * capacity : (d + 1) * capacity] for s in sets], axis=0)
            own.append(part if d == 0 else swap(part, "x", N_X, d))
        own = jnp.concatenate(own, axis=0)
        return own, core_swap(own)

    x_own, x_other = to_owner(row_sets)
    dy_own, dy_other = to_owner(grad_sets)

    hidden_width = down_own.shape[1]
    plain, turned = ((1,), (0,)), ((1,), (1,))
    pre = dot(x_own, gu_own, plain) + dot(x_other, gu_other, plain)
    gate_pre, up_pre = pre[:, :hidden_width], pre[:, hidden_width:]
    sigmoid_gate = jax.nn.sigmoid(gate_pre)
    active = gate_pre * sigmoid_gate
    hidden = (active * up_pre).astype(jnp.bfloat16)
    out_home = feature_sum(dot(hidden, down_own, turned), dot(hidden, down_other, turned), capacity)

    d_hidden = dot(dy_own, down_own, plain) + dot(dy_other, down_other, plain)
    d_gate = d_hidden * up_pre * sigmoid_gate * (1.0 + gate_pre * (1.0 - sigmoid_gate))
    d_gu = jnp.concatenate([d_gate.astype(jnp.bfloat16), (d_hidden * active).astype(jnp.bfloat16)], axis=1)
    dx_home = feature_sum(dot(d_gu, gu_own, turned), dot(d_gu, gu_other, turned), capacity)

    (grad_down,) = weight_grad(dy_own, dy_other, hidden, shard, 1)
    grad_gate, grad_up = weight_grad(x_own, x_other, d_gu, shard, 2)

    home_experts = [jnp.bitwise_xor(z_lo, b) * N_X + jnp.bitwise_xor(x, d) for b in range(2) for d in range(N_X)]
    found = hits(routes, slots_of(routes), home_experts, capacity)
    first, second = (found[:, :, n].astype(jnp.bfloat16) for n in range(2))
    rows = ((0,), (0,))
    layer_out = mix_weights[:, 0:1] * dot(first, out_home, rows) + mix_weights[:, 1:2] * dot(second, out_home, rows)
    grad_tokens = dot(first, dx_home, rows) + dot(second, dx_home, rows)
    return layer_out.astype(jnp.bfloat16), grad_tokens.astype(jnp.bfloat16), grad_gate, grad_up, grad_down


def solution(mesh):
    parts = Mesh(mesh.devices.reshape(2, N_X, 2, 4, 2), EXPERT + SHARD)
    weight_in, weight_out = P(EXPERT, SHARD, None), P(EXPERT, None, SHARD)
    return jax.shard_map(
        local,
        mesh=parts,
        in_specs=(P(EXPERT, SHARD), P(EXPERT, None), P(EXPERT, None), P(EXPERT, SHARD), weight_in, weight_in, weight_in),
        out_specs=(P(EXPERT, SHARD), P(EXPERT, SHARD), weight_out, weight_out, weight_out),
        check_vma=False,
    )
```

```python
import jax
import jax.numpy as jnp
from jax import lax
from jax.experimental import pallas as pl
from jax.experimental.pallas import tpu as pltpu
from jax.sharding import Mesh, PartitionSpec as P


EXPERT = ("z_lo", "x")
SHARD = ("z_hi", "y", "core")
N_X, N_CHIP = 4, 8


def swap(value, axes, size, offset):
    return lax.ppermute(value, axes, [(i, i ^ offset) for i in range(size)])


def chip_swap(value, k):
    return swap(value, ("z_hi", "y"), N_CHIP, k)


def core_swap(value):
    return swap(value, "core", 2, 1)


def dot(a, b, contract):
    return lax.dot_general(a, b, ((contract[0], contract[1]), ((), ())), preferred_element_type=jnp.float32)


def pack(weights, shard):
    rows, hidden = weights[0].shape
    piece = hidden // (2 * N_CHIP)
    step = rows // 2

    def kernel(shard_ref, *refs):
        ins, own, other = refs[:-2], refs[-2], refs[-1]
        chip, core = shard_ref[0] // 2, shard_ref[0] % 2
        for m in range(N_CHIP):
            k = jnp.bitwise_xor(chip, m)
            for out, place in ((own, 2 * m + core), (other, 2 * m + 1 - core)):
                at = pl.ds(pl.multiple_of(place * piece, piece), piece)
                for n, ref in enumerate(ins):
                    out[k, :, n * piece : (n + 1) * piece] = ref[:, at]

    width = piece * len(weights)
    return pl.pallas_call(
        kernel,
        grid_spec=pltpu.PrefetchScalarGridSpec(
            num_scalar_prefetch=1,
            grid=(rows // step,),
            in_specs=[pl.BlockSpec((step, hidden), lambda i, s: (i, 0)) for _ in weights],
            out_specs=[pl.BlockSpec((N_CHIP, step, width), lambda i, s: (0, i, 0))] * 2,
        ),
        out_shape=[jax.ShapeDtypeStruct((N_CHIP, rows, width), weights[0].dtype)] * 2,
        name="pack",
    )(shard, *weights)


def exchange(own, other):
    other = core_swap(other)
    pieces = [jnp.stack([own[k], other[k]]) for k in range(N_CHIP)]
    moved = [pieces[0]] + [chip_swap(pieces[k], k) for k in range(1, N_CHIP)]
    return [jnp.concatenate([m[b] for m in moved], axis=0) for b in range(2)]


def weight_grad(own, other, right, shard, n_out):
    rows, half = own.shape
    piece = half // N_CHIP
    width = right.shape[1] // n_out

    def kernel(shard_ref, own_ref, other_ref, right_ref, *outs):
        core = shard_ref[0] % 2
        for ref, place in ((own_ref, core), (other_ref, 1 - core)):
            total = dot(ref[...], right_ref[...], ((0,), (0,))).astype(outs[0].dtype)
            at = pl.ds(pl.multiple_of(place * piece, piece), piece)
            for n, out in enumerate(outs):
                out[0, at, :] = total[:, n * width : (n + 1) * width]

    in_block = pl.BlockSpec((rows, piece), lambda k, s: (0, k))
    out_block = pl.BlockSpec((1, 2 * piece, width), lambda k, s: (0, jnp.bitwise_xor(s[0] // 2, k), 0))
    return pl.pallas_call(
        kernel,
        grid_spec=pltpu.PrefetchScalarGridSpec(
            num_scalar_prefetch=1,
            grid=(N_CHIP,),
            in_specs=[in_block, in_block, pl.BlockSpec(right.shape, lambda k, s: (0, 0))],
            out_specs=[out_block] * n_out,
        ),
        out_shape=[jax.ShapeDtypeStruct((1, 2 * half, width), jnp.bfloat16)] * n_out,
        cost_estimate=pl.CostEstimate(
            flops=4 * rows * half * right.shape[1],
            bytes_accessed=4 * rows * half + 2 * right.size + 4 * half * right.shape[1],
            transcendentals=0,
        ),
        name="weight_grad",
    )(shard, own, other, right)


def slots_of(routes):
    flat = routes.reshape(-1)
    one_hot = (flat[:, None] == jnp.arange(2 * N_X, dtype=jnp.int32)[None, :]).astype(jnp.int32)
    earlier = jnp.cumsum(one_hot, axis=0) - one_hot
    return jnp.sum(earlier * one_hot, axis=1).reshape(routes.shape)


def hits(routes, slots, experts, capacity):
    row_slot = jnp.tile(jnp.arange(capacity, dtype=jnp.int32), len(experts))
    row_expert = jnp.repeat(jnp.stack(experts), capacity)
    return (row_expert[:, None, None] == routes[None]) & (row_slot[:, None, None] == slots[None])


def feature_sum(own, other, capacity):
    mine = own + core_swap(other.astype(jnp.bfloat16)).astype(jnp.float32)
    piece = own.shape[1] // N_CHIP
    parts = [mine[:, k * piece : (k + 1) * piece] for k in range(N_CHIP)]
    moved = [chip_swap(parts[k].astype(jnp.bfloat16), k) for k in range(1, N_CHIP)]
    total = parts[0]
    for m in moved:
        total = total + m.astype(jnp.float32)
    return send_home(total.astype(jnp.bfloat16), capacity)


def send_home(rows, capacity):
    width = rows.shape[1]
    shaped = rows.reshape(N_X, 2, capacity, width)
    back = [shaped[0]] + [swap(shaped[d], "x", N_X, d) for d in range(1, N_X)]
    back = jnp.stack(back, axis=1)
    crossed = swap(back[1], "z_lo", 2, 1)
    return jnp.concatenate([back[0].reshape(-1, width), crossed.reshape(-1, width)], axis=0)


def local(tokens, routes, mix_weights, cotangent, w_gate, w_up, w_down):
    tok_dev, _ = tokens.shape
    capacity = min(tok_dev, 6 * tok_dev // (2 * N_X))
    z_lo, x = lax.axis_index("z_lo"), lax.axis_index("x")
    shard = lax.axis_index(SHARD).astype(jnp.int32)[None]

    packed_gu = pack([w_gate[0], w_up[0]], shard)
    packed_down = pack([w_down[0]], shard)

    info = jnp.concatenate([routes.astype(jnp.float32), mix_weights], axis=1)
    info_other = swap(info, "z_lo", 2, 1)
    pair = jnp.stack([tokens, cotangent])
    pair_other = swap(pair, "z_lo", 2, 1)
    both = jnp.stack([pair, pair_other])
    gathered = [both] + [chip_swap(both, k) for k in range(1, N_CHIP)]

    gu_own, gu_other = exchange(*packed_gu)
    down_own, down_other = exchange(*packed_down)

    experts = [z_lo * N_X + jnp.bitwise_xor(x, d) for d in range(N_X)]
    row_sets, grad_sets = [], []
    for block, block_info in enumerate((info, info_other)):
        block_routes = block_info[:, :2].astype(jnp.int32)
        found = hits(block_routes, slots_of(block_routes), experts, capacity)
        picker = jnp.any(found, axis=2).astype(jnp.bfloat16)
        weight = jnp.sum(jnp.where(found, block_info[None, :, 2:], 0.0), axis=(1, 2))
        features = [jnp.concatenate([g[block, n] for g in gathered], axis=1) for n in range(2)]
        row_sets.append(dot(picker, features[0], ((1,), (0,))).astype(jnp.bfloat16))
        grad_sets.append((dot(picker, features[1], ((1,), (0,))) * weight[:, None]).astype(jnp.bfloat16))

    def to_owner(sets):
        own = []
        for d in range(N_X):
            part = jnp.concatenate([s[d * capacity : (d + 1) * capacity] for s in sets], axis=0)
            own.append(part if d == 0 else swap(part, "x", N_X, d))
        own = jnp.concatenate(own, axis=0)
        return own, core_swap(own)

    x_own, x_other = to_owner(row_sets)
    dy_own, dy_other = to_owner(grad_sets)

    hidden_width = down_own.shape[1]
    plain, turned = ((1,), (0,)), ((1,), (1,))
    pre = dot(x_own, gu_own, plain) + dot(x_other, gu_other, plain)
    gate_pre, up_pre = pre[:, :hidden_width], pre[:, hidden_width:]
    sigmoid_gate = jax.nn.sigmoid(gate_pre)
    active = gate_pre * sigmoid_gate
    hidden, gate_pre, up_pre = lax.optimization_barrier(((active * up_pre).astype(jnp.bfloat16), gate_pre, up_pre))
    sigmoid_gate = jax.nn.sigmoid(gate_pre)
    active = gate_pre * sigmoid_gate
    out_home = feature_sum(dot(hidden, down_own, turned), dot(hidden, down_other, turned), capacity)

    d_hidden = dot(dy_own, down_own, plain) + dot(dy_other, down_other, plain)
    d_gate = d_hidden * up_pre * sigmoid_gate * (1.0 + gate_pre * (1.0 - sigmoid_gate))
    d_gu = jnp.concatenate([d_gate.astype(jnp.bfloat16), (d_hidden * active).astype(jnp.bfloat16)], axis=1)
    dx_home = feature_sum(dot(d_gu, gu_own, turned), dot(d_gu, gu_other, turned), capacity)

    (grad_down,) = weight_grad(dy_own, dy_other, hidden, shard, 1)
    grad_gate, grad_up = weight_grad(x_own, x_other, d_gu, shard, 2)

    home_experts = [jnp.bitwise_xor(z_lo, b) * N_X + jnp.bitwise_xor(x, d) for b in range(2) for d in range(N_X)]
    found = hits(routes, slots_of(routes), home_experts, capacity)
    first, second = (found[:, :, n].astype(jnp.bfloat16) for n in range(2))
    rows = ((0,), (0,))
    layer_out = mix_weights[:, 0:1] * dot(first, out_home, rows) + mix_weights[:, 1:2] * dot(second, out_home, rows)
    grad_tokens = dot(first, dx_home, rows) + dot(second, dx_home, rows)
    return layer_out.astype(jnp.bfloat16), grad_tokens.astype(jnp.bfloat16), grad_gate, grad_up, grad_down


def solution(mesh):
    parts = Mesh(mesh.devices.reshape(2, N_X, 2, 4, 2), EXPERT + SHARD)
    weight_in, weight_out = P(EXPERT, SHARD, None), P(EXPERT, None, SHARD)
    return jax.shard_map(
        local,
        mesh=parts,
        in_specs=(P(EXPERT, SHARD), P(EXPERT, None), P(EXPERT, None), P(EXPERT, SHARD), weight_in, weight_in, weight_in),
        out_specs=(P(EXPERT, SHARD), P(EXPERT, SHARD), weight_out, weight_out, weight_out),
        check_vma=False,
    )
```

```python
import jax
import jax.numpy as jnp
from jax import lax
from jax.experimental import pallas as pl
from jax.experimental.pallas import tpu as pltpu
from jax.sharding import Mesh, PartitionSpec as P


EXPERT = ("z_lo", "x")
SHARD = ("z_hi", "y", "core")
N_X, N_CHIP = 4, 8


def swap(value, axes, size, offset):
    return lax.ppermute(value, axes, [(i, i ^ offset) for i in range(size)])


def chip_swap(value, k):
    return swap(value, ("z_hi", "y"), N_CHIP, k)


def core_swap(value):
    return swap(value, "core", 2, 1)


def dot(a, b, contract):
    return lax.dot_general(a, b, ((contract[0], contract[1]), ((), ())), preferred_element_type=jnp.float32)


def pack(weights, shard):
    rows, hidden = weights[0].shape
    piece = hidden // (2 * N_CHIP)
    step = rows // 2

    def kernel(shard_ref, *refs):
        ins, outs = refs[: len(weights)], refs[len(weights) :]
        chip, core = shard_ref[0] // 2, shard_ref[0] % 2
        for k, out in enumerate(outs):
            first = 2 * jnp.bitwise_xor(chip, k)
            for b, place in enumerate((first + core, first + 1 - core)):
                at = pl.ds(pl.multiple_of(place * piece, piece), piece)
                for n, ref in enumerate(ins):
                    to = (b * len(weights) + n) * piece
                    out[:, to : to + piece] = ref[:, at]

    width = 2 * piece * len(weights)
    return pl.pallas_call(
        kernel,
        grid_spec=pltpu.PrefetchScalarGridSpec(
            num_scalar_prefetch=1,
            grid=(rows // step,),
            in_specs=[pl.BlockSpec((step, hidden), lambda i, s: (i, 0)) for _ in weights],
            out_specs=[pl.BlockSpec((step, width), lambda i, s: (i, 0))] * N_CHIP,
        ),
        out_shape=[jax.ShapeDtypeStruct((rows, width), weights[0].dtype)] * N_CHIP,
        name="pack",
    )(shard, *weights)


def pack_natural(weight, shard):
    rows, hidden = weight.shape
    piece = hidden // (2 * N_CHIP)
    step = rows // 2

    def kernel(shard_ref, ref, out):
        core = shard_ref[0] % 2
        for chip in range(N_CHIP):
            for b, place in enumerate((2 * chip + core, 2 * chip + 1 - core)):
                at = pl.ds(pl.multiple_of(place * piece, piece), piece)
                out[chip, :, b * piece : (b + 1) * piece] = ref[:, at]

    return pl.pallas_call(
        kernel,
        grid_spec=pltpu.PrefetchScalarGridSpec(
            num_scalar_prefetch=1,
            grid=(rows // step,),
            in_specs=[pl.BlockSpec((step, hidden), lambda i, s: (i, 0))],
            out_specs=pl.BlockSpec((N_CHIP, step, 2 * piece), lambda i, s: (0, i, 0)),
        ),
        out_shape=jax.ShapeDtypeStruct((N_CHIP, rows, 2 * piece), weight.dtype),
        name="pack",
    )(shard, weight)


def chip_exchange(value):
    return lax.all_to_all(value, ("z_hi", "y"), split_axis=0, concat_axis=0, tiled=True)


def exchange(pieces):
    return [pieces[0]] + [chip_swap(pieces[k], k) for k in range(1, N_CHIP)]


def weight_grad(own, other, right, shard, n_out, natural):
    rows, half = own[0].shape
    piece = half // N_CHIP
    width = right.shape[1] // n_out

    def kernel(shard_ref, *refs):
        core = shard_ref[0] % 2
        right_ref, outs = refs[2 * N_X], refs[2 * N_X + 1 :]
        for ins, place in ((refs[:N_X], core), (refs[N_X : 2 * N_X], 1 - core)):
            left = jnp.concatenate([ref[...] for ref in ins], axis=0)
            total = dot(left, right_ref[...], ((0,), (0,))).astype(outs[0].dtype)
            at = pl.ds(pl.multiple_of(place * piece, piece), piece)
            for n, out in enumerate(outs):
                out[0, at, :] = total[:, n * width : (n + 1) * width]

    in_block = pl.BlockSpec((rows, piece), lambda k, s: (0, k))
    out_block = pl.BlockSpec((1, 2 * piece, width), lambda k, s: (0, k if natural else jnp.bitwise_xor(s[0] // 2, k), 0))
    return pl.pallas_call(
        kernel,
        grid_spec=pltpu.PrefetchScalarGridSpec(
            num_scalar_prefetch=1,
            grid=(N_CHIP,),
            in_specs=[in_block] * (2 * N_X) + [pl.BlockSpec(right.shape, lambda k, s: (0, 0))],
            out_specs=[out_block] * n_out,
        ),
        out_shape=[jax.ShapeDtypeStruct((1, 2 * half, width), jnp.bfloat16)] * n_out,
        cost_estimate=pl.CostEstimate(
            flops=4 * N_X * rows * half * right.shape[1],
            bytes_accessed=4 * N_X * rows * half + 2 * right.size + 4 * half * right.shape[1],
            transcendentals=0,
        ),
        name="weight_grad",
    )(shard, *own, *other, right)


def join(first, second, others):
    def kernel(first_ref, second_ref, others_ref, out):
        out[0, 0], out[0, 1] = first_ref[...], second_ref[...]
        out[1] = others_ref[...]

    shape = jax.ShapeDtypeStruct((2, *others.shape), others.dtype)
    return pl.pallas_call(kernel, out_shape=shape, name="join")(first, second, others)


def pick(pieces, which, place, mix, shard, capacity):
    tokens, piece = pieces[0].shape[2:]

    def kernel(shard_ref, place_ref, *refs):
        ins, outs = refs[:N_CHIP], refs[-N_X:]
        chip = shard_ref[0] // 2
        number = lax.broadcasted_iota(jnp.int32, (N_X * capacity, tokens), 0)
        for block in range(2):
            found = [number == place_ref[block, n : n + 1] for n in range(2)]
            picker = jnp.where(found[0] | found[1], 1.0, 0.0).astype(jnp.bfloat16)
            if mix is not None:
                shares = [jnp.where(f, refs[N_CHIP][block, n : n + 1], 0.0) for n, f in enumerate(found)]
                weight = jnp.sum(shares[0] + shares[1], axis=1, keepdims=True)
            for k, ref in enumerate(ins):
                rows = dot(picker, ref[block, which], ((1,), (0,)))
                to = k
                if mix is not None:
                    rows = rows * weight
                    to = jnp.bitwise_xor(chip, k)
                rows = rows.astype(jnp.bfloat16)
                columns = pl.ds(pl.multiple_of(to * piece, piece), piece)
                for d, out in enumerate(outs):
                    out[block * capacity : (block + 1) * capacity, columns] = rows[d * capacity : (d + 1) * capacity]

    extra = [] if mix is None else [mix]
    vmem = pl.BlockSpec(memory_space=pltpu.VMEM)
    return pl.pallas_call(
        kernel,
        in_specs=[pl.BlockSpec(memory_space=pltpu.SMEM)] + [vmem] * (1 + N_CHIP + len(extra)),
        out_specs=[vmem] * N_X,
        out_shape=[jax.ShapeDtypeStruct((2 * capacity, N_CHIP * piece), jnp.bfloat16)] * N_X,
        name="pick",
    )(shard, place, *pieces, *extra)


def split_dot(parts, weights):
    n = len(parts)
    features, width = sum(w.shape[0] for w in weights), weights[0].shape[1]
    rows = sum(p.shape[0] for p in parts)

    def kernel(*refs):
        ins, mine, theirs = refs[: n + len(weights)], refs[-2], refs[-1]
        left = jnp.concatenate([ref[...] for ref in ins[:n]], axis=0)
        right = jnp.concatenate([ref[...] for ref in ins[n:]], axis=0) if len(weights) > 1 else ins[n][...]
        total = dot(left, right, ((1,), (0,)))
        mine[...] = total[:, : width // 2]
        theirs[...] = total[:, width // 2 :]

    assert parts[0].shape[1] == features
    shape = jax.ShapeDtypeStruct((rows, width // 2), jnp.float32)
    return pl.pallas_call(kernel, out_shape=[shape] * 2, name="split_dot")(*parts, *weights)


def row_parts_of(own, other, weight, n):
    rows = own.shape[0] // n

    def kernel(own_ref, other_ref, weight_ref, *outs):
        left = jnp.concatenate([own_ref[...], other_ref[...]], axis=1)
        total = dot(left, weight_ref[...], ((1,), (1,)))
        for d, out in enumerate(outs):
            out[...] = total[d * rows : (d + 1) * rows].astype(out.dtype)

    shape = jax.ShapeDtypeStruct((rows, weight.shape[0]), jnp.bfloat16)
    return pl.pallas_call(kernel, out_shape=[shape] * n, name="row_parts")(own, other, weight)


def parts_of(own, other, pieces):
    def kernel(own_ref, other_ref, *refs):
        left = jnp.concatenate([own_ref[...], other_ref[...]], axis=1)
        for ref, out in zip(refs[: len(pieces)], refs[len(pieces) :], strict=True):
            out[...] = dot(left, ref[...], ((1,), (1,))).astype(out.dtype)

    shape = jax.ShapeDtypeStruct((own.shape[0], pieces[0].shape[0]), jnp.bfloat16)
    return pl.pallas_call(kernel, out_shape=[shape] * len(pieces), name="parts")(own, other, *pieces)


def combine(parts, place, mix):
    capacity, features = parts[0].shape[0] // 2, parts[0].shape[1]
    tokens = mix.shape[1]
    piece = features // N_CHIP

    def kernel(place_ref, mix_ref, *refs):
        ins, out = refs[:-1], refs[-1]
        number = lax.broadcasted_iota(jnp.int32, (N_X * capacity, tokens), 0)
        for block in range(2):
            rows = jnp.concatenate([ref[block * capacity : (block + 1) * capacity] for ref in ins], axis=0)
            total = jnp.zeros((tokens, features), jnp.float32)
            for n in range(2):
                chosen = jnp.where(number == place_ref[block, n : n + 1], 1.0, 0.0).astype(jnp.bfloat16)
                total = total + mix_ref[block, :, n : n + 1] * dot(chosen, rows, ((0,), (0,)))
            total = total.astype(out.dtype)
            for chip in range(N_CHIP):
                out[chip, block] = total[:, chip * piece : (chip + 1) * piece]

    shape = jax.ShapeDtypeStruct((N_CHIP, 2, tokens, piece), jnp.bfloat16)
    return pl.pallas_call(kernel, out_shape=shape, name="combine")(place, mix, *parts)


def finish(own, crossed, place):
    rows, width = own.shape

    def kernel(place_ref, own_ref, crossed_ref, out):
        tokens = out.shape[0]
        number = lax.broadcasted_iota(jnp.int32, (rows, tokens), 0)
        total = jnp.zeros(out.shape, jnp.float32)
        for b, ref in enumerate((own_ref, crossed_ref)):
            here = [number + b * rows == place_ref[n : n + 1] for n in range(2)]
            total = total + dot(jnp.where(here[0] | here[1], 1.0, 0.0).astype(jnp.bfloat16), ref[...], ((0,), (0,)))
        out[...] = total.astype(out.dtype)

    shape = jax.ShapeDtypeStruct((place.shape[1], width), jnp.bfloat16)
    return pl.pallas_call(kernel, out_shape=shape, name="finish")(place, own, crossed)


def slots_of(routes):
    flat = routes.reshape(-1)
    one_hot = (flat[:, None] == jnp.arange(2 * N_X, dtype=jnp.int32)[None, :]).astype(jnp.int32)
    earlier = jnp.cumsum(one_hot, axis=0) - one_hot
    return jnp.sum(earlier * one_hot, axis=1).reshape(routes.shape)


def feature_sum(own, other, pieces, capacity):
    half = N_CHIP // 2
    parts = parts_of(own, other, pieces[1 : half + 1]) + parts_of(own, other, pieces[half + 1 :] + pieces[:1])
    total = parts[-1].astype(jnp.float32)
    for k in range(1, N_CHIP):
        total = total + chip_swap(parts[k - 1], k).astype(jnp.float32)
    return send_home(total.astype(jnp.bfloat16), capacity)


def send_home(rows, capacity):
    width = rows.shape[1]
    shaped = rows.reshape(N_X, 2, capacity, width)
    back = [shaped[0]] + [swap(shaped[d], "x", N_X, d) for d in range(1, N_X)]
    back = jnp.stack(back, axis=1)
    crossed = swap(back[1], "z_lo", 2, 1)
    return back[0].reshape(-1, width), crossed.reshape(-1, width)


def local(tokens, routes, mix_weights, cotangent, w_gate, w_up, w_down):
    tok_dev, _ = tokens.shape
    capacity = min(tok_dev, 6 * tok_dev // (2 * N_X))
    z_lo, x = lax.axis_index("z_lo"), lax.axis_index("x")
    shard = lax.axis_index(SHARD).astype(jnp.int32)[None]

    packed_gu = pack([w_gate[0], w_up[0]], shard)
    packed_down = pack_natural(w_down[0], shard)

    routes_other, mix_other = swap(routes, "z_lo", 2, 1), swap(mix_weights, "z_lo", 2, 1)
    pair = jnp.stack([tokens, cotangent])
    pair_other = swap(pair, "z_lo", 2, 1)
    both = join(tokens, cotangent, pair_other)
    gathered = [both] + [chip_swap(both, k) for k in range(1, N_CHIP)]

    gu_pieces = exchange(packed_gu)
    down = chip_exchange(packed_down)
    down = down.reshape(-1, down.shape[2])

    homes, places = [], []
    for block_routes in (routes, routes_other):
        row = jnp.bitwise_xor(block_routes % N_X, x) * capacity + slots_of(block_routes)
        homes.append((row + jnp.bitwise_xor(block_routes // N_X, z_lo) * N_X * capacity).T)
        places.append(jnp.where(homes[-1] < N_X * capacity, homes[-1], 2 * N_X * capacity))
    home, place = homes[0], jnp.stack(places)
    mix_both = jnp.stack([mix_weights, mix_other])
    mix_turned = jnp.stack([mix_weights.T, mix_other.T])

    def to_owner(parts):
        moved = [parts[0]] + [swap(parts[d], "x", N_X, d) for d in range(1, N_X)]
        return moved, [core_swap(part) for part in moved]

    row_parts = pick(gathered, 0, place, None, shard, capacity)
    grad_parts = pick(gathered, 1, place, mix_turned, shard, capacity)
    x_own, x_other = to_owner(row_parts)
    dy_own, dy_other = to_owner(grad_parts)

    width = down.shape[1] // 2

    def features_dot(parts, weights):
        mine, theirs = split_dot(parts, weights)
        theirs = core_swap(theirs)
        return mine + theirs

    pre = features_dot(x_own, gu_pieces)
    gate_pre, up_pre = pre[:, :width], pre[:, width:]
    hidden = (gate_pre * jax.nn.sigmoid(gate_pre) * up_pre).astype(jnp.bfloat16)
    hidden, gate_pre, up_pre = lax.optimization_barrier((hidden, gate_pre, up_pre))
    sigmoid_gate = jax.nn.sigmoid(gate_pre)
    active = gate_pre * sigmoid_gate
    hidden_other = core_swap(hidden)
    out_parts = row_parts_of(hidden, hidden_other, down, N_X)
    out_parts = [out_parts[0]] + [swap(out_parts[d], "x", N_X, d) for d in range(1, N_X)]
    by_chip = combine(out_parts, place, mix_both)
    by_chip = chip_exchange(by_chip)
    out_tokens = jnp.sum(by_chip.astype(jnp.float32), axis=0)
    out_crossed = swap(out_tokens[1].astype(jnp.bfloat16), "z_lo", 2, 1)
    layer_out = out_tokens[0] + out_crossed.astype(jnp.float32)

    d_hidden = features_dot(dy_own, [down])
    d_gate = d_hidden * up_pre * sigmoid_gate * (1.0 + gate_pre * (1.0 - sigmoid_gate))
    d_gu = jnp.concatenate([d_gate.astype(jnp.bfloat16), (d_hidden * active).astype(jnp.bfloat16)], axis=1)
    dx_home = feature_sum(d_gu, core_swap(d_gu), gu_pieces, capacity)

    (grad_down,) = weight_grad(dy_own, dy_other, hidden, shard, 1, True)
    grad_gate, grad_up = weight_grad(x_own, x_other, d_gu, shard, 2, False)

    grad_tokens = finish(*dx_home, home)
    return layer_out.astype(jnp.bfloat16), grad_tokens, grad_gate, grad_up, grad_down


def solution(mesh):
    parts = Mesh(mesh.devices.reshape(2, N_X, 2, 4, 2), EXPERT + SHARD)
    weight_in, weight_out = P(EXPERT, SHARD, None), P(EXPERT, None, SHARD)
    return jax.shard_map(
        local,
        mesh=parts,
        in_specs=(P(EXPERT, SHARD), P(EXPERT, None), P(EXPERT, None), P(EXPERT, SHARD), weight_in, weight_in, weight_in),
        out_specs=(P(EXPERT, SHARD), P(EXPERT, SHARD), weight_out, weight_out, weight_out),
        check_vma=False,
    )
```

```python
import jax
import jax.numpy as jnp
from jax import lax
from jax.experimental import pallas as pl
from jax.experimental.pallas import tpu as pltpu
from jax.sharding import Mesh, PartitionSpec as P


EXPERT = ("z_lo", "x")
SHARD = ("z_hi", "y", "core")
N_X, N_CHIP = 4, 8


def swap(value, axes, size, offset):
    return lax.ppermute(value, axes, [(i, i ^ offset) for i in range(size)])


def chip_swap(value, k):
    return swap(value, ("z_hi", "y"), N_CHIP, k)


def core_swap(value):
    return swap(value, "core", 2, 1)


def dot(a, b, contract):
    return lax.dot_general(a, b, ((contract[0], contract[1]), ((), ())), preferred_element_type=jnp.float32)


def pack(weights, shard):
    rows, hidden = weights[0].shape
    piece = hidden // (2 * N_CHIP)
    step = rows // 2

    def kernel(shard_ref, *refs):
        ins, outs = refs[: len(weights)], refs[len(weights) :]
        chip, core = shard_ref[0] // 2, shard_ref[0] % 2
        for k, out in enumerate(outs):
            first = 2 * jnp.bitwise_xor(chip, k)
            for b, place in enumerate((first + core, first + 1 - core)):
                at = pl.ds(pl.multiple_of(place * piece, piece), piece)
                for n, ref in enumerate(ins):
                    to = (b * len(weights) + n) * piece
                    out[:, to : to + piece] = ref[:, at]

    width = 2 * piece * len(weights)
    return pl.pallas_call(
        kernel,
        grid_spec=pltpu.PrefetchScalarGridSpec(
            num_scalar_prefetch=1,
            grid=(rows // step,),
            in_specs=[pl.BlockSpec((step, hidden), lambda i, s: (i, 0)) for _ in weights],
            out_specs=[pl.BlockSpec((step, width), lambda i, s: (i, 0))] * N_CHIP,
        ),
        out_shape=[jax.ShapeDtypeStruct((rows, width), weights[0].dtype)] * N_CHIP,
        name="pack",
    )(shard, *weights)


def pack_natural(weight, shard):
    rows, hidden = weight.shape
    piece = hidden // (2 * N_CHIP)
    step = rows // 2

    def kernel(shard_ref, ref, out):
        core = shard_ref[0] % 2
        for chip in range(N_CHIP):
            for b, place in enumerate((2 * chip + core, 2 * chip + 1 - core)):
                at = pl.ds(pl.multiple_of(place * piece, piece), piece)
                out[chip, :, b * piece : (b + 1) * piece] = ref[:, at]

    return pl.pallas_call(
        kernel,
        grid_spec=pltpu.PrefetchScalarGridSpec(
            num_scalar_prefetch=1,
            grid=(rows // step,),
            in_specs=[pl.BlockSpec((step, hidden), lambda i, s: (i, 0))],
            out_specs=pl.BlockSpec((N_CHIP, step, 2 * piece), lambda i, s: (0, i, 0)),
        ),
        out_shape=jax.ShapeDtypeStruct((N_CHIP, rows, 2 * piece), weight.dtype),
        name="pack",
    )(shard, weight)


def chip_exchange(value):
    return lax.all_to_all(value, ("z_hi", "y"), split_axis=0, concat_axis=0, tiled=True)


def exchange(pieces):
    return [pieces[0]] + [chip_swap(pieces[k], k) for k in range(1, N_CHIP)]


def weight_grad(own, other, right, shard, n_out, natural):
    rows, half = own[0].shape
    piece = half // N_CHIP
    width = right.shape[1] // n_out

    def kernel(shard_ref, *refs):
        chip, core = shard_ref[0] // 2, shard_ref[0] % 2
        right_ref, outs = refs[2 * N_X], refs[2 * N_X + 1 :]
        sides = [jnp.concatenate([ref[...] for ref in refs[i * N_X : (i + 1) * N_X]], axis=0) for i in range(2)]
        total = dot(jnp.concatenate(sides, axis=1), right_ref[...], ((0,), (0,))).astype(outs[0].dtype)
        for side, place in enumerate((core, 1 - core)):
            for j in range(2):
                to = 2 * (j if natural else jnp.bitwise_xor(j, chip % 2)) + place
                at = pl.ds(pl.multiple_of(to * piece, piece), piece)
                start = (2 * side + j) * piece
                for n, out in enumerate(outs):
                    out[0, at, :] = total[start : start + piece, n * width : (n + 1) * width]

    def out_index(k, s):
        return 0, k if natural else jnp.bitwise_xor(s[0] // 4, k), 0

    in_block = pl.BlockSpec((rows, 2 * piece), lambda k, s: (0, k))
    out_block = pl.BlockSpec((1, 4 * piece, width), out_index)
    return pl.pallas_call(
        kernel,
        grid_spec=pltpu.PrefetchScalarGridSpec(
            num_scalar_prefetch=1,
            grid=(N_CHIP // 2,),
            in_specs=[in_block] * (2 * N_X) + [pl.BlockSpec(right.shape, lambda k, s: (0, 0))],
            out_specs=[out_block] * n_out,
        ),
        out_shape=[jax.ShapeDtypeStruct((1, 2 * half, width), jnp.bfloat16)] * n_out,
        cost_estimate=pl.CostEstimate(
            flops=4 * N_X * rows * half * right.shape[1],
            bytes_accessed=4 * N_X * rows * half + 2 * right.size + 4 * half * right.shape[1],
            transcendentals=0,
        ),
        name="weight_grad",
    )(shard, *own, *other, right)


def join(first, second, others):
    def kernel(first_ref, second_ref, others_ref, out):
        out[0, 0], out[0, 1] = first_ref[...], second_ref[...]
        out[1] = others_ref[...]

    shape = jax.ShapeDtypeStruct((2, *others.shape), others.dtype)
    return pl.pallas_call(kernel, out_shape=shape, name="join")(first, second, others)


def pick(pieces, which, place, mix, shard, capacity):
    tokens, piece = pieces[0].shape[2:]

    def kernel(shard_ref, place_ref, *refs):
        ins, outs = refs[:N_CHIP], refs[-N_X:]
        chip = shard_ref[0] // 2
        number = lax.broadcasted_iota(jnp.int32, (N_X * capacity, tokens), 0)
        for block in range(2):
            found = [number == place_ref[block, n : n + 1] for n in range(2)]
            picker = jnp.where(found[0] | found[1], 1.0, 0.0).astype(jnp.bfloat16)
            if mix is not None:
                shares = [jnp.where(f, refs[N_CHIP][block, n : n + 1], 0.0) for n, f in enumerate(found)]
                weight = jnp.sum(shares[0] + shares[1], axis=1, keepdims=True)
            for k, ref in enumerate(ins):
                rows = dot(picker, ref[block, which], ((1,), (0,)))
                to = k
                if mix is not None:
                    rows = rows * weight
                    to = jnp.bitwise_xor(chip, k)
                rows = rows.astype(jnp.bfloat16)
                columns = pl.ds(pl.multiple_of(to * piece, piece), piece)
                for d, out in enumerate(outs):
                    out[block * capacity : (block + 1) * capacity, columns] = rows[d * capacity : (d + 1) * capacity]

    extra = [] if mix is None else [mix]
    vmem = pl.BlockSpec(memory_space=pltpu.VMEM)
    return pl.pallas_call(
        kernel,
        in_specs=[pl.BlockSpec(memory_space=pltpu.SMEM)] + [vmem] * (1 + N_CHIP + len(extra)),
        out_specs=[vmem] * N_X,
        out_shape=[jax.ShapeDtypeStruct((2 * capacity, N_CHIP * piece), jnp.bfloat16)] * N_X,
        name="pick",
    )(shard, place, *pieces, *extra)


def split_dot(parts, weights):
    n = len(parts)
    features, width = sum(w.shape[0] for w in weights), weights[0].shape[1]
    rows = sum(p.shape[0] for p in parts)

    def kernel(*refs):
        ins, mine, theirs = refs[: n + len(weights)], refs[-2], refs[-1]
        left = jnp.concatenate([ref[...] for ref in ins[:n]], axis=0)
        right = jnp.concatenate([ref[...] for ref in ins[n:]], axis=0) if len(weights) > 1 else ins[n][...]
        total = dot(left, right, ((1,), (0,)))
        mine[...] = total[:, : width // 2]
        theirs[...] = total[:, width // 2 :]

    assert parts[0].shape[1] == features
    shape = jax.ShapeDtypeStruct((rows, width // 2), jnp.float32)
    return pl.pallas_call(kernel, out_shape=[shape] * 2, name="split_dot")(*parts, *weights)


def row_parts_of(own, other, weight, n):
    rows = own.shape[0] // n

    def kernel(own_ref, other_ref, weight_ref, *outs):
        left = jnp.concatenate([own_ref[...], other_ref[...]], axis=1)
        total = dot(left, weight_ref[...], ((1,), (1,)))
        for d, out in enumerate(outs):
            out[...] = total[d * rows : (d + 1) * rows].astype(out.dtype)

    shape = jax.ShapeDtypeStruct((rows, weight.shape[0]), jnp.bfloat16)
    return pl.pallas_call(kernel, out_shape=[shape] * n, name="row_parts")(own, other, weight)


def parts_of(own, other, pieces):
    def kernel(own_ref, other_ref, *refs):
        left = jnp.concatenate([own_ref[...], other_ref[...]], axis=1)
        for ref, out in zip(refs[: len(pieces)], refs[len(pieces) :], strict=True):
            out[...] = dot(left, ref[...], ((1,), (1,))).astype(out.dtype)

    shape = jax.ShapeDtypeStruct((own.shape[0], pieces[0].shape[0]), jnp.bfloat16)
    return pl.pallas_call(kernel, out_shape=[shape] * len(pieces), name="parts")(own, other, *pieces)


def combine(parts, place, mix):
    capacity, features = parts[0].shape[0] // 2, parts[0].shape[1]
    tokens = mix.shape[2]
    piece = features // N_CHIP

    def kernel(place_ref, mix_ref, *refs):
        ins, out = refs[:-1], refs[-1]
        number = lax.broadcasted_iota(jnp.int32, (N_X * capacity, tokens), 0)
        square = (tokens, tokens)
        same = lax.broadcasted_iota(jnp.int32, square, 0) == lax.broadcasted_iota(jnp.int32, square, 1)
        for block in range(2):
            rows = jnp.concatenate([ref[block * capacity : (block + 1) * capacity] for ref in ins], axis=0)
            total = jnp.zeros((tokens, features), jnp.float32)
            for n in range(2):
                chosen = jnp.where(number == place_ref[block, n : n + 1], 1.0, 0.0).astype(jnp.bfloat16)
                share = jnp.sum(jnp.where(same, mix_ref[block, n : n + 1], 0.0), axis=1, keepdims=True)
                total = total + share * dot(chosen, rows, ((0,), (0,)))
            total = total.astype(out.dtype)
            for chip in range(N_CHIP):
                out[chip, block] = total[:, chip * piece : (chip + 1) * piece]

    shape = jax.ShapeDtypeStruct((N_CHIP, 2, tokens, piece), jnp.bfloat16)
    return pl.pallas_call(kernel, out_shape=shape, name="combine")(place, mix, *parts)


def finish(own, crossed, place):
    rows, width = own.shape

    def kernel(place_ref, own_ref, crossed_ref, out):
        tokens = out.shape[0]
        number = lax.broadcasted_iota(jnp.int32, (rows, tokens), 0)
        total = jnp.zeros(out.shape, jnp.float32)
        for b, ref in enumerate((own_ref, crossed_ref)):
            here = [number + b * rows == place_ref[n : n + 1] for n in range(2)]
            total = total + dot(jnp.where(here[0] | here[1], 1.0, 0.0).astype(jnp.bfloat16), ref[...], ((0,), (0,)))
        out[...] = total.astype(out.dtype)

    shape = jax.ShapeDtypeStruct((place.shape[1], width), jnp.bfloat16)
    return pl.pallas_call(kernel, out_shape=shape, name="finish")(place, own, crossed)


def slots_of(routes):
    flat = routes.reshape(-1)
    one_hot = (flat[:, None] == jnp.arange(2 * N_X, dtype=jnp.int32)[None, :]).astype(jnp.int32)
    earlier = jnp.cumsum(one_hot, axis=0) - one_hot
    return jnp.sum(earlier * one_hot, axis=1).reshape(routes.shape)


def feature_sum(own, other, pieces, capacity):
    half = N_CHIP // 2
    far = parts_of(own, other, pieces[half : half + 2]) + parts_of(own, other, pieces[half + 2 :])
    near = parts_of(own, other, pieces[:half])
    total = near[0].astype(jnp.float32)
    for k in range(1, N_CHIP):
        total = total + chip_swap((near + far)[k], k).astype(jnp.float32)
    return send_home(total.astype(jnp.bfloat16), capacity)


def send_home(rows, capacity):
    width = rows.shape[1]
    shaped = rows.reshape(N_X, 2, capacity, width)
    back = [shaped[0]] + [swap(shaped[d], "x", N_X, d) for d in range(1, N_X)]
    back = jnp.stack(back, axis=1)
    crossed = swap(back[1], "z_lo", 2, 1)
    return back[0].reshape(-1, width), crossed.reshape(-1, width)


def local(tokens, routes, mix_weights, cotangent, w_gate, w_up, w_down):
    tok_dev, _ = tokens.shape
    capacity = min(tok_dev, 6 * tok_dev // (2 * N_X))
    z_lo, x = lax.axis_index("z_lo"), lax.axis_index("x")
    shard = lax.axis_index(SHARD).astype(jnp.int32)[None]

    packed_gu = pack([w_gate[0], w_up[0]], shard)
    packed_down = pack_natural(w_down[0], shard)

    routes_other, mix_other = swap(routes, "z_lo", 2, 1), swap(mix_weights, "z_lo", 2, 1)
    pair = jnp.stack([tokens, cotangent])
    pair_other = swap(pair, "z_lo", 2, 1)
    both = join(tokens, cotangent, pair_other)
    gathered = [both] + [chip_swap(both, k) for k in range(1, N_CHIP)]

    gu_pieces = exchange(packed_gu)
    down = chip_exchange(packed_down)
    down = down.reshape(-1, down.shape[2])

    homes, places = [], []
    for block_routes in (routes, routes_other):
        row = jnp.bitwise_xor(block_routes % N_X, x) * capacity + slots_of(block_routes)
        homes.append((row + jnp.bitwise_xor(block_routes // N_X, z_lo) * N_X * capacity).T)
        places.append(jnp.where(homes[-1] < N_X * capacity, homes[-1], 2 * N_X * capacity))
    home, place = homes[0], jnp.stack(places)
    mix_turned = jnp.stack([mix_weights.T, mix_other.T])

    def to_owner(parts):
        moved = [parts[0]]
        for d in range(1, N_X):
            moved.append(swap(parts[d], "x", N_X, d))
        return moved, [core_swap(part) for part in moved]

    row_parts = pick(gathered, 0, place, None, shard, capacity)
    grad_parts = pick(gathered, 1, place, mix_turned, shard, capacity)
    x_own, x_other = to_owner(row_parts)
    dy_own, dy_other = to_owner(grad_parts)

    width = down.shape[1] // 2

    def features_dot(parts, weights):
        mine, theirs = split_dot(parts, weights)
        theirs = core_swap(theirs)
        return mine + theirs

    pre = features_dot(x_own, gu_pieces)
    gate_pre, up_pre = pre[:, :width], pre[:, width:]
    hidden = (gate_pre * jax.nn.sigmoid(gate_pre) * up_pre).astype(jnp.bfloat16)
    hidden, gate_pre, up_pre = lax.optimization_barrier((hidden, gate_pre, up_pre))
    sigmoid_gate = jax.nn.sigmoid(gate_pre)
    active = gate_pre * sigmoid_gate
    hidden_other = core_swap(hidden)
    out_parts = row_parts_of(hidden, hidden_other, down, N_X)
    out_parts = [out_parts[0]] + [swap(out_parts[d], "x", N_X, d) for d in range(1, N_X)]
    by_chip = combine(out_parts, place, mix_turned)
    by_chip = chip_exchange(by_chip)
    out_tokens = jnp.sum(by_chip.astype(jnp.float32), axis=0)
    out_crossed = swap(out_tokens[1].astype(jnp.bfloat16), "z_lo", 2, 1)
    layer_out = out_tokens[0] + out_crossed.astype(jnp.float32)

    d_hidden = features_dot(dy_own, [down])
    d_gate = d_hidden * up_pre * sigmoid_gate * (1.0 + gate_pre * (1.0 - sigmoid_gate))
    d_gu = jnp.concatenate([d_gate.astype(jnp.bfloat16), (d_hidden * active).astype(jnp.bfloat16)], axis=1)
    dx_home = feature_sum(d_gu, core_swap(d_gu), gu_pieces, capacity)

    (grad_down,) = weight_grad(dy_own, dy_other, hidden, shard, 1, True)
    grad_gate, grad_up = weight_grad(x_own, x_other, d_gu, shard, 2, False)

    grad_tokens = finish(*dx_home, home)
    return layer_out.astype(jnp.bfloat16), grad_tokens, grad_gate, grad_up, grad_down


def solution(mesh):
    parts = Mesh(mesh.devices.reshape(2, N_X, 2, 4, 2), EXPERT + SHARD)
    weight_in, weight_out = P(EXPERT, SHARD, None), P(EXPERT, None, SHARD)
    return jax.shard_map(
        local,
        mesh=parts,
        in_specs=(P(EXPERT, SHARD), P(EXPERT, None), P(EXPERT, None), P(EXPERT, SHARD), weight_in, weight_in, weight_in),
        out_specs=(P(EXPERT, SHARD), P(EXPERT, SHARD), weight_out, weight_out, weight_out),
        check_vma=False,
    )
```
